32 devices in a mesh: dp: 8 (over z, y), tensor: 4 (over x, core).
Axes of the slice: x: 2, y: 2, z: 4, core: 2. Of those that a mesh axis runs over, the one named last changes fastest.
Arguments:
- frames: float32 [8, 512, 512], P('dp'), may hold values from -6 to 6
- masked_frames: int32 [8, 256], P('dp'), may hold values from 0 to 511, as said below
- distractors: int32 [8, 256, 100], P('dp'), may hold values from 0 to 511, as said below
- code_ids: int32 [8, 512, 2], P('dp'), may hold values from 0 to 319
- feature_weight: float32 [512, 768], replicated, may hold values from -0.25 to 0.25
- conv_weight: float32 [128, 48, 768], P(None, None, 'tensor'), may hold values from -0.078125 to 0.078125
- qkv_weight: float32 [768, 3, 768], P(None, None, 'tensor'), may hold values from -0.21875 to 0.21875
- out_weight: float32 [768, 768], P('tensor'), may hold values from -1.75 to 1.75
- up_weight: float32 [768, 3072], P(None, 'tensor'), may hold values from -0.21875 to 0.21875
- down_weight: float32 [3072, 768], P('tensor'), may hold values from -0.109375 to 0.109375
- hidden_proj: float32 [768, 256], replicated, may hold values from -0.21875 to 0.21875
- target_proj: float32 [256, 256], replicated, may hold values from -0.375 to 0.375
- codebook: float32 [2, 320, 128], replicated, may hold values from -6 to 6
- quant_weight: float32 [512, 640], replicated, may hold values from -0.25 to 0.25
- norm_gains: float32 [3, 768], replicated, may hold values from 0.5 to 1.5
- shared_bias: float32 [7, 768], replicated, may hold values from -3 to 3
- split_bias: float32 [3, 768], P(None, 'tensor'), may hold values from -3 to 3
- up_bias: float32 [3072], P('tensor'), may hold values from -3 to 3
- feature_norm: float32 [2, 512], replicated, may hold values from 0.5 to 1.5
- head_bias: float32 [2, 256], replicated, may hold values from -3 to 3
- quant_bias: float32 [640], replicated, may hold values from -4 to 4
- momentum: float32 [4, 4025280], P('tensor', 'dp'), may hold values from -6 to 6
- error_buffer: float32 [8, 4, 4014080], P('dp', 'tensor'), may hold values from -4 to 4
- factors: float32 [4, 8, 5120], P('tensor'), may hold values from -6 to 6
Outputs:
- loss: float32 [], replicated
- new_momentum: float32 [4, 4025280], P('tensor', 'dp')
- update: float32 [4, 4025280], P('tensor', 'dp')
- new_error: float32 [8, 4, 4014080], P('dp', 'tensor')
- new_factors: float32 [4, 8, 5120], P('tensor')
The draws below stay inside these ranges and needn't reach their ends.
Inputs may be any that keep to these rules, and one draw needn't show every extreme that they name: `masked_frames`: the 256 masked frames of a clip are distinct. `distractors`: each distractor names a frame of the same clip other than the masked frame it belongs to; a frame may repeat.
All inputs are finite; a program needn't handle non-finite values.
Results may differ from the reference program's by a relative error of at most 0.0003.
Values sent between devices are 32-bit elements; how exact they have to be, the bound alone decides.
No kernel may reach another device: no remote copies, remote signals or barrier semaphores. Data moves between devices by JAX's collectives and lax.ppermute only.
A program may use at most 384 MiB of HBM per device.

```python
import jax
import jax.numpy as jnp
from jax import lax

D = 768
HDIM = 64
FF = 3072
CH = 512
KERNEL = 128
CODES = 320
GROUPS = 2
CVDIM = 256
PROJ = 256
NEG = 100
RANK = 8
SEQ = 512
MASKED = 256
CLIPS_DEV = 1
CLIPS = 8
CG = 48
CV = 128
MATFLAT = 4014080
FLAT = 4025280
QROWS = 5120
N_DP = 8
N_TENSOR = 4


def masked_rows(key):
    clip_keys = jax.random.split(jax.random.fold_in(key, 17), CLIPS)

    def one_clip(clip_key):
        return jax.random.permutation(clip_key, SEQ)[:MASKED].astype(jnp.int32)
    return jax.vmap(one_clip)(clip_keys)


def draw_masked_frames(key, part):
    return masked_rows(key)


def draw_distractors(key, part):
    masked = masked_rows(key)
    offsets = jax.random.randint(jax.random.fold_in(key, 29), (CLIPS, MASKED, NEG), 0, SEQ - 1)
    return (offsets + (offsets >= masked[:, :, None]).astype(jnp.int32)).astype(jnp.int32)


def set_ends(values, rng, least, high):
    place = [jax.random.randint(jax.random.fold_in(rng, axis), (), 0, length) for axis, length in enumerate(values.shape)]
    main_axis = values.shape.index(max(values.shape))
    next_to = place[:main_axis] + [(place[main_axis] + 1) % values.shape[main_axis]] + place[main_axis + 1:]
    return values.at[tuple(place)].set(least).at[tuple(next_to)].set(high)


def levels(rng, dims, cuts, least, top_value):
    level, own = 1.0, jax.random.fold_in(rng, 6)
    for dim, shards_of in cuts:
        steps = jnp.exp(jax.random.uniform(jax.random.fold_in(own, dim), (shards_of,), jnp.float32, least / len(cuts), top_value / len(cuts)))
        level = level * jnp.repeat(steps, dims[dim] // shards_of).reshape([-1 if axis == dim else 1 for axis in range(len(dims))])
    return level


def normal_values(key, dims, deviation, reach, shards=(), kind=jnp.bfloat16):
    result = deviation * jax.random.normal(key, dims, jnp.float32)
    if shards:
        result = result * levels(key, dims, shards, -0.22, 0.18)
    return jnp.clip(result, -reach, reach).astype(kind)


def setup_inputs(seed: int = 0) -> dict:
    key_list = jax.random.split(jax.random.key(seed), 25)
    frames = normal_values(key_list[0], (CLIPS, SEQ, CH), 1.0, 6.0, ((0, 8),), jnp.float32)
    masked_frames = draw_masked_frames(jax.random.fold_in(key_list[24], 71), 0)
    distractors = draw_distractors(jax.random.fold_in(key_list[24], 71), 0)
    code_ids = set_ends(jax.random.randint(key_list[3], (CLIPS, SEQ, GROUPS), 0, CODES), jax.random.fold_in(key_list[3], 1), 0, CODES - 1).astype(jnp.int32)
    feature_weight = normal_values(key_list[4], (CH, D), CH ** -0.5, 0.25, (), jnp.float32)
    conv_weight = normal_values(key_list[5], (KERNEL, CG, D), (KERNEL * CG) ** -0.5, 0.078125, ((2, 4),), jnp.float32)
    qkv_weight = normal_values(key_list[6], (D, 3, D), D ** -0.5, 0.21875, ((2, 4),), jnp.float32)
    out_weight = normal_values(key_list[7], (D, D), (D * 8 // SEQ) ** -0.5, 1.75, ((0, 4),), jnp.float32)
    up_weight = normal_values(key_list[8], (D, FF), D ** -0.5, 0.21875, ((1, 4),), jnp.float32)
    down_weight = normal_values(key_list[9], (FF, D), FF ** -0.5, 0.109375, ((0, 4),), jnp.float32)
    hidden_proj = normal_values(key_list[10], (D, PROJ), D ** -0.5, 0.21875, (), jnp.float32)
    target_proj = normal_values(key_list[11], (CVDIM, PROJ), CVDIM ** -0.5, 0.375, (), jnp.float32)
    codebook = normal_values(key_list[12], (GROUPS, CODES, CV), 1.0, 6.0, (), jnp.float32)
    quant_weight = normal_values(key_list[13], (CH, GROUPS * CODES), CH ** -0.5, 0.25, (), jnp.float32)
    norm_gains = jnp.clip(1.0 + 0.1 * jax.random.normal(key_list[14], (3, D), jnp.float32), 0.5, 1.5)
    shared_bias = normal_values(key_list[15], (7, D), 0.5, 3.0, (), jnp.float32)
    split_bias = normal_values(key_list[16], (3, D), 0.5, 3.0, ((1, 4),), jnp.float32)
    up_bias = normal_values(key_list[17], (FF,), 0.5, 3.0, ((0, 4),), jnp.float32)
    feature_norm = jnp.clip(1.0 + 0.1 * jax.random.normal(key_list[18], (2, CH), jnp.float32), 0.5, 1.5)
    head_bias = normal_values(key_list[19], (2, PROJ), 0.5, 3.0, (), jnp.float32)
    quant_bias = normal_values(key_list[20], (GROUPS * CODES,), 1.0, 4.0, (), jnp.float32)
    momentum = normal_values(key_list[21], (N_TENSOR, FLAT), 1.0, 6.0, ((0, 4), (1, 8)), jnp.float32)
    error_buffer = normal_values(key_list[22], (N_DP, N_TENSOR, MATFLAT), 0.5, 4.0, ((0, 8), (1, 4)), jnp.float32)
    factors = normal_values(key_list[23], (N_TENSOR, RANK, QROWS), 1.0, 6.0, ((0, 4),), jnp.float32)
    return dict(frames=frames, masked_frames=masked_frames, distractors=distractors, code_ids=code_ids, feature_weight=feature_weight, conv_weight=conv_weight, qkv_weight=qkv_weight, out_weight=out_weight, up_weight=up_weight, down_weight=down_weight, hidden_proj=hidden_proj, target_proj=target_proj, codebook=codebook, quant_weight=quant_weight, norm_gains=norm_gains, shared_bias=shared_bias, split_bias=split_bias, up_bias=up_bias, feature_norm=feature_norm, head_bias=head_bias, quant_bias=quant_bias, momentum=momentum, error_buffer=error_buffer, factors=factors)


highest = lax.Precision.HIGHEST
norm_eps = 1e-05
cos_eps = 1e-06
log_eps = 1e-07
logit_divisor = 0.1
diversity_weight = 0.1
momentum_decay = 0.9
step_rate = 0.001

@jax.custom_vjp
def low(v):
    return lax.optimization_barrier(v.astype(jnp.bfloat16)).astype(jnp.float32)

@jax.custom_vjp
def low_back(v):
    return v

def low_keep(v):
    return (low(v), None)

def low_pass(kept, grad):
    return (grad,)

def back_keep(v):
    return (v, None)

def back_low(kept, grad):
    return (low(grad),)
low.defvjp(low_keep, low_pass)
low_back.defvjp(back_keep, back_low)

def exact_array_multiply(left, right):
    return jnp.dot(left.astype(jnp.float32), right.astype(jnp.float32), precision=highest, preferred_element_type=jnp.float32)

def gelu_exact(values):
    return jax.nn.gelu(values, approximate=False)

def layer_norm(values, gain, shift):
    average = lax.optimization_barrier(jnp.mean(values, axis=-1, keepdims=True))
    centered = values - average
    feature_variance = lax.optimization_barrier(jnp.mean(centered * centered, axis=-1, keepdims=True))
    return centered * lax.rsqrt(feature_variance + norm_eps) * gain + shift

def position_conv(hidden, kernel):
    length, model_width = hidden.shape
    taps, group_channel_width, _ = kernel.shape
    groups = model_width // group_channel_width
    padded = jnp.pad(hidden, ((taps // 2, taps // 2 - 1), (0, 0))).reshape(length + taps - 1, groups, group_channel_width)

    def one_tap(running, tap_index):
        window = lax.dynamic_slice_in_dim(padded, tap_index, length, 0)
        tap_weight = lax.dynamic_index_in_dim(kernel, tap_index, 0, keepdims=False).reshape(group_channel_width, groups, group_channel_width)
        return (running + jnp.einsum('tgi,igj->tgj', window, tap_weight, precision=highest), None)
    initial = jnp.zeros((length, groups, group_channel_width), jnp.float32)
    running, _ = lax.scan(one_tap, initial, jnp.arange(taps, dtype=jnp.int32))
    return running.reshape(length, model_width)

def quantized(code_ids, codebook):
    entries = codebook.shape[1]
    pieces = []
    for group_id in range(codebook.shape[0]):
        onehot = (code_ids[:, group_id][:, None] == jnp.arange(entries, dtype=jnp.int32)[None, :]).astype(jnp.float32)
        pieces.append(exact_array_multiply(onehot, codebook[group_id]))
    return jnp.concatenate(pieces, axis=-1)

def contrast(predicted, target, masked, negatives):
    length = predicted.shape[0]
    positions = jnp.arange(length, dtype=jnp.int32)
    picked = (masked[:, None] == positions[None, :]).astype(jnp.float32)
    chosen = exact_array_multiply(picked, predicted)
    guessed_direction_rows = chosen * lax.rsqrt(lax.optimization_barrier(jnp.sum(chosen * chosen, axis=-1, keepdims=True)) + cos_eps)
    quantized_direction_rows = target * lax.rsqrt(lax.optimization_barrier(jnp.sum(target * target, axis=-1, keepdims=True)) + cos_eps)
    cosine_logit_table = exact_array_multiply(guessed_direction_rows, quantized_direction_rows.T) / logit_divisor
    candidates = jnp.concatenate([masked[:, None], negatives], axis=1).astype(jnp.int32)
    logits = jnp.take_along_axis(cosine_logit_table, candidates, axis=1)
    return jnp.sum(jax.nn.logsumexp(logits, axis=-1) - logits[:, 0])

def diversity_term(prob_total, masked_total):
    mean_probs = (prob_total / masked_total).reshape(GROUPS, CODES)
    perplexity = jnp.sum(jnp.exp(-lax.optimization_barrier(jnp.sum(mean_probs * jnp.log(mean_probs + log_eps), axis=-1))))
    return diversity_weight * masked_total * (GROUPS * CODES - perplexity) / (GROUPS * CODES)

def orthonormal(left):
    gram = jnp.dot(left.T, left, precision=highest)
    lower = jnp.linalg.cholesky(gram)
    return jax.scipy.linalg.solve_triangular(lower, left.T, lower=True).T

def clip_terms(params, frames, masked, negatives, code_ids):
    length = frames.shape[0]
    positions = jnp.arange(length, dtype=jnp.int32)
    picked = (masked[:, None] == positions[None, :]).astype(jnp.float32)
    is_masked = lax.optimization_barrier(jnp.sum(picked, axis=0))[:, None]
    normed = layer_norm(frames, params['feature_norm'][0], params['feature_norm'][1])
    hidden = exact_array_multiply(normed, params['feature_weight']) + params['shared_bias'][1]
    hidden = hidden * (1.0 - is_masked) + is_masked * params['shared_bias'][0]
    conv_out = gelu_exact(position_conv(hidden, params['conv_weight']) + params['split_bias'][0])
    state = layer_norm(hidden + conv_out, params['norm_gains'][0], params['shared_bias'][2])
    model_width = state.shape[1]
    heads = model_width // HDIM
    projected = exact_array_multiply(state, params['qkv_weight'].reshape(model_width, 3 * model_width)).reshape(length, 3, model_width)
    queries = (projected[:, 0] + params['split_bias'][1]).reshape(length, heads, HDIM)
    keys_all = projected[:, 1].reshape(length, heads, HDIM)
    values_all = (projected[:, 2] + params['split_bias'][2]).reshape(length, heads, HDIM)
    scores = jnp.einsum('shd,thd->hst', queries, keys_all, precision=highest) * HDIM ** (-0.5)
    weights = jax.nn.softmax(scores, axis=-1)
    mixed = jnp.einsum('hst,thd->shd', weights, values_all, precision=highest).reshape(length, model_width)
    state = layer_norm(state + exact_array_multiply(mixed, params['out_weight']) + params['shared_bias'][3], params['norm_gains'][1], params['shared_bias'][4])
    inner = gelu_exact(exact_array_multiply(state, params['up_weight']) + params['up_bias'])
    state = layer_norm(state + exact_array_multiply(inner, params['down_weight']) + params['shared_bias'][5], params['norm_gains'][2], params['shared_bias'][6])
    predicted = exact_array_multiply(state, params['hidden_proj']) + params['head_bias'][0]
    target = exact_array_multiply(quantized(code_ids, params['codebook']), params['target_proj']) + params['head_bias'][1]
    loss_sum = contrast(predicted, target, masked, negatives)
    logits = (exact_array_multiply(normed, params['quant_weight']) + params['quant_bias']).reshape(length, GROUPS, CODES)
    probs = jax.nn.softmax(logits, axis=-1).reshape(length, GROUPS * CODES)
    return (loss_sum, lax.optimization_barrier(jnp.sum(is_masked * probs, axis=0)))

def reference(frames, masked_frames, distractors, code_ids, feature_weight, conv_weight, qkv_weight, out_weight, up_weight, down_weight, hidden_proj, target_proj, codebook, quant_weight, norm_gains, shared_bias, split_bias, up_bias, feature_norm, head_bias, quant_bias, momentum, error_buffer, factors):
    params = {'feature_weight': feature_weight, 'conv_weight': conv_weight, 'qkv_weight': qkv_weight, 'out_weight': out_weight, 'up_weight': up_weight, 'down_weight': down_weight, 'hidden_proj': hidden_proj, 'target_proj': target_proj, 'codebook': codebook, 'quant_weight': quant_weight, 'norm_gains': norm_gains, 'shared_bias': shared_bias, 'split_bias': split_bias, 'up_bias': up_bias, 'feature_norm': feature_norm, 'head_bias': head_bias, 'quant_bias': quant_bias}
    params_all = jax.tree.map(lambda leaf: jnp.broadcast_to(leaf, (N_DP,) + leaf.shape), params)

    def grouped(array):
        return array.reshape((N_DP, CLIPS_DEV) + array.shape[1:])
    inputs = (grouped(frames), grouped(masked_frames), grouped(distractors), grouped(code_ids))
    masked_total = MASKED * CLIPS_DEV * N_DP

    def objective_of(per_group):

        def one_group(items):
            group_params = items[0]

            def one_clip(clip_items):
                return jax.checkpoint(clip_terms)(group_params, *clip_items)
            loss_each, prob_each = lax.map(one_clip, items[1:])
            return (jnp.sum(loss_each), lax.optimization_barrier(jnp.sum(prob_each, axis=0)))
        loss_groups, prob_groups = lax.map(one_group, (per_group,) + inputs)
        return jnp.sum(loss_groups) + diversity_term(lax.optimization_barrier(jnp.sum(prob_groups, axis=0)), masked_total)
    objective, pullback = jax.vjp(objective_of, params_all)
    grads, = pullback(jnp.ones_like(objective))
    loss = objective / masked_total
    width = D // N_TENSOR
    hidden_width = FF // N_TENSOR
    moms_out, updates_out, errors_out, factors_out = ([], [], [], [])
    for tensor_rank in range(N_TENSOR):
        lower_col = tensor_rank * width
        upper_col = lower_col + width
        lower_hid = tensor_rank * hidden_width
        upper_hid = lower_hid + hidden_width
        matrices = [grads['feature_weight'], grads['conv_weight'][:, :, :, lower_col:upper_col].reshape(N_DP, KERNEL * CG, width), grads['qkv_weight'][:, :, :, lower_col:upper_col].reshape(N_DP, D, 3 * width), grads['out_weight'][:, lower_col:upper_col, :], grads['up_weight'][:, :, lower_hid:upper_hid], grads['down_weight'][:, lower_hid:upper_hid, :], grads['hidden_proj'], grads['target_proj'], grads['codebook'].reshape(N_DP, GROUPS * CODES, CV), grads['quant_weight']]
        vectors = jnp.concatenate([grads['norm_gains'].reshape(N_DP, -1), grads['shared_bias'].reshape(N_DP, -1), grads['split_bias'][:, :, lower_col:upper_col].reshape(N_DP, -1), grads['up_bias'][:, lower_hid:upper_hid], grads['feature_norm'].reshape(N_DP, -1), grads['head_bias'].reshape(N_DP, -1), grads['quant_bias']], axis=1)
        approx_flat, error_flat, right_parts = ([], [], [])
        error_at = 0
        factor_at = 0
        for matrix in matrices:
            height, breadth = (matrix.shape[1], matrix.shape[2])
            cells = height * breadth
            corrected = matrix + error_buffer[:, tensor_rank, error_at:error_at + cells].reshape(N_DP, height, breadth)
            previous = factors[tensor_rank, :, factor_at:factor_at + breadth].T
            left = lax.optimization_barrier(jnp.sum(jnp.einsum('nab,bk->nak', corrected, previous, precision=highest), axis=0))
            orth_basis = orthonormal(left)
            right = lax.optimization_barrier(jnp.sum(jnp.einsum('nab,ak->nbk', corrected, orth_basis, precision=highest), axis=0)) / N_DP
            approx = jnp.dot(orth_basis, right.T, precision=highest)
            approx_flat.append(approx.reshape(-1))
            error_flat.append((corrected - approx[None]).reshape(N_DP, -1))
            right_parts.append(right.T)
            error_at += cells
            factor_at += breadth
        grad_flat = jnp.concatenate(approx_flat + [lax.optimization_barrier(jnp.sum(vectors, axis=0)) / N_DP])
        moved = momentum_decay * momentum[tensor_rank] + grad_flat
        moms_out.append(moved)
        updates_out.append(-step_rate * moved)
        errors_out.append(jnp.concatenate(error_flat, axis=1))
        factors_out.append(jnp.concatenate(right_parts, axis=1))
    return (loss, jnp.stack(moms_out), jnp.stack(updates_out), jnp.stack(errors_out, axis=1), jnp.stack(factors_out))
```

```python
import jax, functools
import jax.numpy as jnp
from jax import lax
from jax.experimental import pallas as pl
from jax.experimental.pallas import tpu as pltpu
f32=jnp.float32; bf=jnp.bfloat16
NN=((1,),(0,)); NT=((1,),(1,)); TN=((0,),(0,))
def split(x):
    hi=x.astype(bf); return hi,(x-hi.astype(f32)).astype(bf)
def d(a,b,dims): return lax.dot_general(a,b,(dims,((),())),preferred_element_type=f32)
def d3(a,b,dims): return d(a[0],b[0],dims)+(d(a[0],b[1],dims)+d(a[1],b[0],dims))
def iota(shape,ax): return lax.broadcasted_iota(jnp.int32,shape,ax)
def roll(x,s): return pltpu.roll(x,s%128,1)
def m8(x,n=8): return pl.multiple_of(x,n)

def sel_own(rank, width):
    c=iota((width,256),0); n=iota((width,256),1)
    g=n//64; i=n-g*64
    return jnp.where((i<48)&(c==rank*192+g*48+i),1.0,0.0).astype(bf)

def lane_low(n): return iota((n,128),1)<64

def prep_w8(w_ref, w8h, w8l):
    w8h[...]=jnp.zeros_like(w8h); w8l[...]=jnp.zeros_like(w8l)
    low=lane_low(48); l32=iota((48,128),1)
    def body(m,c):
        for j in range(8):
            def pieces(b, off):
                r=pl.ds(m8((m*16+b)*48,16),48)
                a=w_ref[r,0:128]; z=jnp.concatenate([w_ref[r,128:192],jnp.zeros((48,64),f32)],axis=1)
                g0=roll(a,off) if off else a
                g1=roll(a,off-48)
                g2=jnp.where((l32>=off)&(l32<off+32),roll(a,off-96),roll(z,off+32))
                g3=roll(z,off-16)
                return g0,g1,g2,g3
            ev=pieces(2*j,0); od=pieces(2*j+1,64)
            for g in range(4):
                v=jnp.where(low,ev[g],od[g])
                h,l=split(v)
                w8h[g,pl.ds(m8(m*64,16),48),j*128:(j+1)*128]=h
                w8l[g,pl.ds(m8(m*64,16),48),j*128:(j+1)*128]=l
        return c
    lax.fori_loop(0,8,body,0)

def place_pairs(x64, xp):
    low=lane_low(512)
    for t in range(2):
        a=x64[:,t*128:(t+1)*128]; r=roll(a,64)
        z=jnp.zeros_like(a)
        for g,(lo,hi) in ((2*t,(a,r)),(2*t+1,(r,a))):
            xp[2*g,64:576,:]=jnp.where(low,lo,z).astype(bf)
            xp[2*g+1,64:576,:]=jnp.where(low,z,hi).astype(bf)

def zero_pad(xp):
    xp[:,0:64,:]=jnp.zeros((8,64,128),bf); xp[:,576:640,:]=jnp.zeros((8,64,128),bf)

def build_col(xp, g, col):
    for j in range(4):
        col[:,j*128:(j+1)*128]=xp[2*g,32*j:32*j+528,:]+xp[2*g+1,32*j+16:32*j+544,:]

def to_natural(parts):
    n=parts[0].shape[0]; l=iota((n,128),1)
    r2=roll(parts[2],96)
    t0=jnp.where(l<48,parts[0],jnp.where(l<96,roll(parts[1],48),r2))
    t1=jnp.where(l<16,r2,roll(parts[3],16))
    return t0,t1[:,:64]

def conv_fwd_kernel(rank_ref, hid_ref, w_ref, bias_ref, pre_ref, out_ref, w8h, w8l, xph, xpl, colh, coll, y, acc):
    prep_w8(w_ref,w8h,w8l)
    sel=sel_own(rank_ref[0],768)
    h,l=split(hid_ref[...])
    zero_pad(xph); zero_pad(xpl)
    place_pairs(d(h,sel,NN),xph); place_pairs(d(l,sel,NN),xpl)
    low=lane_low(512)
    for g in range(4):
        build_col(xph,g,colh); build_col(xpl,g,coll)
        def body(i,c):
            r=pl.ds(m8(i*176,16),176)
            y[r,:]=d3((colh[r,:],coll[r,:]),(w8h[g],w8l[g]),NN)
            return c
        lax.fori_loop(0,3,body,0)
        u=jnp.zeros((512,128),f32); v=u
        for j in range(8):
            u=u+y[2*j:2*j+512,j*128:(j+1)*128]
            v=v+y[2*j+1:2*j+513,j*128:(j+1)*128]
        acc[g]=u+roll(v,64)
    t0,t1=to_natural([acc[g] for g in range(4)])
    pre0=t0+bias_ref[0:1,0:128]; pre1=t1+bias_ref[0:1,128:192]
    pre_ref[:,0:128]=pre0; pre_ref[:,128:192]=pre1
    ge=lambda v: 0.5*v*(1.0+lax.erf(v*0.7071067811865476))
    out_ref[:,0:128]=ge(pre0); out_ref[:,128:192]=ge(pre1)

V=pltpu.VMEM; SM=pl.BlockSpec(memory_space=pltpu.SMEM)
VM=pl.BlockSpec(memory_space=pltpu.VMEM)
def conv_fwd(rank, hidden, w2, bias):
    return pl.pallas_call(conv_fwd_kernel,
        out_shape=(jax.ShapeDtypeStruct((512,192),f32),)*2+(jax.ShapeDtypeStruct((4,512,1024),bf),)*2,
        in_specs=[SM,VM,VM,VM], out_specs=(VM,)*4,
        scratch_shapes=[V((8,640,128),bf)]*2+[V((528,512),bf)]*2+[V((528,1024),f32),V((4,512,128),f32)],
        compiler_params=pltpu.CompilerParams(vmem_limit_bytes=12*2**20),name="conv_fwd")(rank,hidden,w2,bias)

def from_natural(t0, t1):
    n=t0.shape[0]; l=iota((n,128),1)
    z=jnp.concatenate([t1,jnp.zeros((n,64),f32)],axis=1)
    return t0, roll(t0,-48), jnp.where(l<32,roll(t0,-96),roll(z,32)), roll(z,-16)

def gelu_grad(u):
    return 0.5*(1.0+lax.erf(u*0.7071067811865476))+u*jnp.exp(-0.5*u*u)*0.3989422804014327
MATS=[("feature",512,768),("conv",6144,192),("qkv",768,576),("out",192,768),("up",768,768),("down",768,768),("hproj",768,256),("tproj",256,256),("book",640,128),("quant",512,640)]
class Mat: pass
def plan():
    res={}; fo=0; po=0; qo=0
    for n,r,c in MATS:
        m=Mat(); m.name=n; m.rows=r; m.cols=c; m.pair=(c%128!=0)
        m.w=(2*c if m.pair else c)//128
        m.R=r//2 if m.pair else r
        m.nrow=m.R*m.w
        m.flat=fo; fo+=m.nrow
        m.p=po; po+=r+(-r)%128
        m.q=qo; qo+=c
        m.rb=256 if m.R%256==0 else (128 if m.R%128==0 else m.R)
        m.nb=m.R//m.rb
        res[n]=m
    return res,fo,po,qo
PL,FROWS,PCOLS,QCOLS=plan()

def shifted_tile(fac, start, t, n):
    a=start+128*t
    if a%128==0: return fac[:,a:a+128]
    low=iota((n,128),1)<64
    b=a-64
    x=roll(fac[:,b:b+128],64)
    y=roll(fac[:,b+128:b+256],64) if b+256<=fac.shape[1] else x
    return jnp.where(low,x,y)

def mat_tiles(fac, m):
    n=8; low=iota((8,128),1)<64; z=jnp.zeros((8,128),f32)
    if not m.pair: return [fac[:,m.q+128*t:m.q+128*t+128] for t in range(m.w)]
    h=(m.w-1)//2
    nat=[shifted_tile(fac,m.q,t,8) for t in range(h)]
    last=shifted_tile(fac,m.q,h,8)
    ev=nat+[jnp.where(low,last,z)]+[z]*h
    ro=[roll(x,64) for x in nat]+[roll(last,64)]
    od=[z]*h+[jnp.where(low,z,ro[0])]+[jnp.where(low,ro[t-1],ro[t]) for t in range(1,h+1)]
    return [jnp.concatenate([e,o],axis=0) for e,o in zip(ev,od)]

def untile(tiles, m):
    if not m.pair: return tiles
    low=iota((8,128),1)<64
    h=(m.w-1)//2
    ev=[t[0:8] for t in tiles[:h+1]]
    ro=[roll(t[8:16],64) for t in tiles[h:]]
    od=[jnp.where(low,ro[t],ro[t+1]) for t in range(h)]+[ro[h]]
    return [a+b for a,b in zip(ev,od)]

def m_tiles(mref, m, r0, tmp):
    rb=m.rb
    if not m.pair: return lambda q: mref[pl.ds(r0,rb),q*128:(q+1)*128]
    h=(m.w-1)//2; low=iota((rb,128),1)<64
    r2=pl.ds(pl.multiple_of(2*r0,8),2*rb)
    for t in range(h):
        tmp[t,0:2*rb,:]=mref[r2,t*128:(t+1)*128]
    tmp[h,0:2*rb,0:64]=mref[r2,h*128:h*128+64]
    def part(par,t): return tmp[t,pl.ds(par,rb,stride=2),:]
    def get(q):
        if q<h: return part(0,q)
        t=q-h
        if t==0: return jnp.where(low,part(0,h),roll(part(1,0),64))
        return jnp.where(low,roll(part(1,t-1),64),roll(part(1,t),64))
    return get

def left_kernel(names, nvec, *refs):
    n=len(names)
    fac_ref,e_ref=refs[0:2]; vr=refs[2:2+nvec]; ms=refs[2+nvec:2+nvec+n]; c_ref,p_ref=refs[2+nvec+n:4+nvec+n]; fsc,tmp,sem=refs[4+nvec+n:]
    base=[]; b=0; pb=[]; p=0
    for x in names:
        m=PL[x]; base.append(b); b+=m.nrow; pb.append(p); p+=m.rows+(-m.rows)%128
    cps=[]
    for i,x in enumerate(names):
        m=PL[x]
        ce=pltpu.make_async_copy(e_ref.at[pl.ds(m.flat,m.nrow)],c_ref.at[pl.ds(base[i],m.nrow)],sem.at[i]); ce.start()
        cps.append(ce)
    fac=fac_ref[...]
    if nvec: pack_vectors(vr,p_ref,p)
    for i,x in enumerate(names):
        m=PL[x]
        qt=[split(t) for t in mat_tiles(fac,m)]
        k=qt[0][0].shape[0]
        for t,(qh,ql) in enumerate(qt):
            fsc[0:2*k,t*128:(t+1)*128]=jnp.concatenate([qh,ql],axis=0)
        cps[i].wait()
        rb=m.rb
        def body(ib,carry):
            r0=ib*rb
            get=m_tiles(ms[i],m,pl.multiple_of(r0,8),tmp)
            acc=jnp.zeros((2*k,rb),f32); acc2=jnp.zeros((k,rb),f32)
            for q in range(m.w):
                sl=pl.ds(base[i]+r0*m.w+q,rb,stride=m.w) if m.w>1 else pl.ds(pl.multiple_of(base[i]+r0,8),rb)
                v=c_ref[sl,:]+get(q)
                c_ref[sl,:]=v
                vh,vl=split(v)
                f=fsc[0:2*k,q*128:(q+1)*128]
                acc=acc+d(f,vh,NT); acc2=acc2+d(f[0:k],vl,NT)
            r=acc[0:k]+acc[k:2*k]+acc2
            if m.pair:
                p_ref[:,pl.ds(pl.multiple_of(pb[i]+r0,128),rb)]=r[0:8]
                p_ref[:,pl.ds(pl.multiple_of(pb[i]+m.R+r0,128),rb)]=r[8:16]
            elif m.nb==1:
                p_ref[:,pb[i]:pb[i]+rb]=r
            else:
                p_ref[:,pl.ds(pl.multiple_of(pb[i]+r0,128),rb)]=r
            return carry
        lax.fori_loop(0,m.nb,body,0)
        if m.rows%128:
            a=pb[i]+m.rows; p_ref[:,a:a+(-m.rows)%128]=jnp.zeros((8,(-m.rows)%128),f32)

ANY=pl.BlockSpec(memory_space=pltpu.HBM)
VCOLS=11*128
def pack_vectors(vr, p_ref, col):
    v0,v1,v2,gm,gcb,qb,ub,fn,hb0,hb1,gqb,lp=vr
    row=[0]
    def put(t):
        a,b=divmod(row[0],8); p_ref[b:b+1,col+128*a:col+128*a+128]=t; row[0]+=1
    def puts(x):
        for i in range(x.shape[1]//128): put(x[:,128*i:128*i+128])
    for x in (v0[0:1,:],v1[0:1,:],v2[0:1,:],gm[0:1,:],gm[1:2,:],v0[1:2,:],v1[2:3,:],v1[1:2,:],v2[2:3,:],v2[1:2,:]): puts(x)
    puts(jnp.concatenate([gcb[...],qb[:,0:192],qb[:,384:576],ub[...],fn[0:1,:],fn[1:2,:],hb0[...],hb1[...],gqb[...],jnp.broadcast_to(lp[...],(1,64))],axis=1))
def left(names, fac, eflat, ms, vecs=()):
    n=len(names); rows=sum(PL[x].nrow for x in names); pc=sum(PL[x].rows+(-PL[x].rows)%128 for x in names)
    return pl.pallas_call(functools.partial(left_kernel,names,len(vecs)),
        out_shape=(jax.ShapeDtypeStruct((rows,128),f32),jax.ShapeDtypeStruct((8,pc+(VCOLS if vecs else 0)),f32)),
        in_specs=[VM,ANY]+[VM]*(len(vecs)+n), out_specs=(VM,VM),
        scratch_shapes=[V((32,1152),bf),V((5,512,128),f32),pltpu.SemaphoreType.DMA((n,))],
        compiler_params=pltpu.CompilerParams(vmem_limit_bytes=5*2**20),name="left")(fac,eflat,*vecs,*ms)

def orth_all(flat, bh_ref, bl_ref):
    gs=[]
    for x,pr,o,po,n in flat:
        v=pr[:,o:o+n]
        gs.append(lax.dot_general(v,v,(NT,((),())),precision=lax.Precision.HIGHEST,preferred_element_type=f32))
    k=len(flat)
    a=jnp.stack(gs)
    e=(iota((8,8),0)==iota((8,8),1)).astype(f32)
    a=jnp.concatenate([a,jnp.broadcast_to(e[None],(k,8,8))],axis=2)
    ri=lax.broadcasted_iota(jnp.int32,(k,8,1),1)
    ds=[]
    for j in range(8):
        piv=a[:,j:j+1,j:j+1]; row=a[:,j:j+1,:]; col=a[:,:,j:j+1]
        ds.append(piv)
        a=a-jnp.where(ri>j,col/piv,0.0)*row
    dg=jnp.concatenate(ds,axis=1)
    li=a[:,:,8:16]*lax.rsqrt(dg)
    for i,(x,pr,o,po,n) in enumerate(flat):
        b=lax.dot_general(li[i],pr[:,o:o+n],(NN,((),())),precision=lax.Precision.HIGHEST,preferred_element_type=f32)
        h,l=split(b); bh_ref[:,po:po+n]=h; bl_ref[:,po:po+n]=l

def right_kernel(names, nc, *refs):
    ps=refs[0:nc]; cs=refs[nc:2*nc]; bh_ref,bl_ref,r_ref,acc=refs[2*nc:]
    p_all=[(pr,g) for pr,g in zip(ps,names)]
    po=0; qo=0; flat=[]
    for pr,g in p_all:
        o=0
        for x in g:
            m=PL[x]; n=m.rows+(-m.rows)%128; flat.append((x,pr,o,po,n)); o+=n; po+=n
    orth_all(flat,bh_ref,bl_ref)
    po=0
    for gi,g in enumerate(names):
        base=0
        for x in g:
            m=PL[x]; rb=m.rb; k=16 if m.pair else 8; c_ref=cs[gi]
            acc[...]=jnp.zeros_like(acc)
            def body(ib,carry):
                r0=ib*rb
                def bas(ref):
                    if m.pair: return jnp.concatenate([ref[:,pl.ds(pl.multiple_of(po+r0,128),rb)],ref[:,pl.ds(pl.multiple_of(po+m.R+r0,128),rb)]],axis=0)
                    if m.nb==1: return ref[:,po:po+rb]
                    return ref[:,pl.ds(pl.multiple_of(po+r0,128),rb)]
                h=bas(bh_ref); l=bas(bl_ref)
                hl=jnp.concatenate([h,l],axis=0)
                for q in range(m.w):
                    sl=pl.ds(base+r0*m.w+q,rb,stride=m.w) if m.w>1 else pl.ds(pl.multiple_of(base+r0,8),rb)
                    vh,vl=split(c_ref[sl,:])
                    x1=d(hl,vh,NN); x2=d(h,vl,NN)
                    acc[0:k,q*128:(q+1)*128]+=x1[0:k]+x1[k:2*k]+x2
                return carry
            lax.fori_loop(0,m.nb,body,0)
            tiles=untile([acc[0:k,q*128:(q+1)*128] for q in range(m.w)],m)
            for t,v in enumerate(tiles):
                r_ref[:,qo+t*128:qo+(t+1)*128]=v
            po+=m.rows+(-m.rows)%128; qo+=len(tiles)*128; base+=m.nrow

def qpad(x): return PL[x].cols+(-PL[x].cols)%128
def right(names, psums, cs):
    fl=[x for g in names for x in g]; pc=sum(PL[x].rows+(-PL[x].rows)%128 for x in fl); qc=sum(qpad(x) for x in fl); nc=len(cs)
    return pl.pallas_call(functools.partial(right_kernel,names,nc),
        out_shape=(jax.ShapeDtypeStruct((8,pc),bf),jax.ShapeDtypeStruct((8,pc),bf),jax.ShapeDtypeStruct((8,qc),f32)),
        in_specs=[VM]*(2*nc), out_specs=(VM,)*3,
        scratch_shapes=[V((16,1152),f32)],
        compiler_params=pltpu.CompilerParams(vmem_limit_bytes=5*2**20),name="right")(*psums,*cs)

BLK=1536
def sizes(share_len):
    srows=-(-share_len//128); return srows+(-srows)%8
def final_kernel(names, share_len, srows, ndp, last, di_ref, *refs):
    ng=len(names)
    bh_ref,bl_ref,rs_ref=refs[0:3]; cs=refs[3:3+ng]; refs=refs[3+ng:]
    if last:
        rs1_ref,names1,vec_ref,vcol,div_ref,mom_ref,_,share_in=refs[0],last[0],refs[1],last[1],refs[2],refs[3],refs[4],refs[5]
        ne_ref,nf_ref,loss_ref,nm_ref,up_ref=refs[6:11]; share,rsc,nfs,buf,sem_o,mom,nmb,upb,sem_m=refs[11:]
    else:
        ne_ref,share=refs[0:2]; rsc,nfs,buf,sem_o=refs[2:]
    start=di_ref[0]*share_len
    base0=start//128; s=start-base0*128; sub=base0%8; basea=base0-sub
    if last:
        cm=pltpu.make_async_copy(mom_ref,mom,sem_m.at[0]); cm.start()
        cs2=pltpu.make_async_copy(share_in,share,sem_m.at[3]); cs2.start()
        loss_ref[...]=(vec_ref[7:8,vcol+10*128+64:vcol+10*128+65]+div_ref[...])*(1.0/(256*ndp))
    def natural(ref, fl, out):
        o=0
        for x in fl:
            m=PL[x]; nt=qpad(x)//128
            ts=[ref[:,o+128*t:o+128*t+128]*(1.0/ndp) for t in range(nt)]; o+=qpad(x)
            if m.q%128:
                ro=[roll(t,64) for t in ts]; low8=iota((8,128),1)<64; q0=m.q-64
                out[:,q0+64:q0+128]=ro[0][:,64:128]
                for t in range(1,nt): out[:,q0+128*t:q0+128*t+128]=jnp.where(low8,ro[t-1],ro[t])
            elif m.cols%128:
                for t in range(nt-1): out[:,m.q+128*t:m.q+128*t+128]=ts[t]
                out[:,m.q+128*(nt-1):m.q+128*(nt-1)+64]=ts[-1][:,0:64]
            else:
                for t in range(nt): out[:,m.q+128*t:m.q+128*t+128]=ts[t]
    fl=[x for g in names for x in g]
    nfs[...]=jnp.zeros_like(nfs)
    natural(rs_ref,fl,nfs)
    fac=nfs[...]
    po=0; outs=[]; bo=0
    for gi,g in enumerate(names):
        base=0; c_ref=cs[gi]
        for x in g:
            m=PL[x]; rb=m.rb; k=16 if m.pair else 8; idx=len(outs)
            for t,v in enumerate(mat_tiles(fac,m)):
                h,l=split(v)
                rsc[idx%2,0:3*k,t*128:(t+1)*128]=jnp.concatenate([h,l,h],axis=0)
            def lhs_of(r0):
                def bas(ref):
                    if m.pair: return jnp.concatenate([ref[:,pl.ds(pl.multiple_of(po+r0,128),rb)],ref[:,pl.ds(pl.multiple_of(po+m.R+r0,128),rb)]],axis=0)
                    if m.nb==1: return ref[:,po:po+rb]
                    return ref[:,pl.ds(pl.multiple_of(po+r0,128),rb)]
                h=bas(bh_ref).astype(f32); l=bas(bl_ref).astype(f32)
                return jnp.concatenate([h,h,l],axis=0).T.astype(bf)
            def body(ib,carry):
                r0=ib*rb; row0=r0*m.w
                lhs=lhs_of(r0)
                for q in range(m.w):
                    ci=pl.ds(base+row0+q,rb,stride=m.w) if m.w>1 else pl.ds(pl.multiple_of(base+row0,8),rb)
                    bi=pl.ds(bo+row0+q,rb,stride=m.w) if m.w>1 else pl.ds(pl.multiple_of(bo+row0,8),rb)
                    buf[bi,:]=c_ref[ci,:]-d(lhs,rsc[idx%2,0:3*k,q*128:(q+1)*128],NN)
                pltpu.make_async_copy(buf.at[pl.ds(pl.multiple_of(bo+row0,8),rb*m.w)],ne_ref.at[pl.ds(pl.multiple_of(m.flat+row0,8),rb*m.w)],sem_o.at[idx]).start()
                return carry
            lax.fori_loop(0,m.nb,body,0)
            def sbody(ib,carry):
                r0=ib*rb; row0=m.flat+r0*m.w
                @pl.when((row0+rb*m.w>basea)&(row0<basea+srows+8))
                def _():
                    lhs=lhs_of(r0)
                    o=BLK+row0-basea
                    for q in range(m.w):
                        sl=pl.ds(o+q,rb,stride=m.w) if m.w>1 else pl.ds(pl.multiple_of(o,8),rb)
                        share[sl,:]=d(lhs,rsc[idx%2,0:3*k,q*128:(q+1)*128],NN)
                return carry
            if last and idx==0: cs2.wait()
            lax.fori_loop(0,m.nb,sbody,0)
            outs.append(pltpu.make_async_copy(buf.at[pl.ds(bo,m.nrow)],ne_ref.at[pl.ds(m.flat,m.nrow)],sem_o.at[idx]))
            po+=m.rows+(-m.rows)%128; base+=m.nrow; bo+=m.nrow
    if last:
        nf_ref[...]=jnp.zeros_like(nf_ref)
        natural(rs1_ref,names1,nf_ref); natural(rs_ref,fl,nf_ref)
        @pl.when((FROWS+88>basea)&(FROWS<basea+srows+8))
        def _():
            for a in range(11):
                share[pl.ds(pl.multiple_of(BLK+FROWS-basea+8*a,8),8),:]=vec_ref[:,vcol+128*a:vcol+128*a+128]*(1.0/ndp)
        cm.wait()
        l=iota((8,128),1); sh=(128-s)%128
        def part(i):
            o=BLK+sub+i*8
            return jnp.where(l<128-s,pltpu.roll(share[pl.ds(o,8),:],sh,1),pltpu.roll(share[pl.ds(o+1,8),:],sh,1)).reshape(1,1024)
        def step(i):
            c=pl.ds(pl.multiple_of(i*1024,1024),1024)
            nm=0.9*mom[:,c]+part(i)
            nmb[:,c]=nm; upb[:,c]=-0.001*nm
        nfull=share_len//1024; u=8
        def sh_body(i,carry):
            for j in range(u): step(i*u+j)
            return carry
        lax.fori_loop(0,nfull//u,sh_body,0)
        for j in range(nfull-nfull%u,nfull): step(j)
        t=nfull*1024; r=share_len-t
        if r:
            nm=0.9*mom[:,t:t+r]+part(nfull)[:,:r]
            nmb[:,t:t+r]=nm; upb[:,t:t+r]=-0.001*nm
        c1=pltpu.make_async_copy(nmb,nm_ref,sem_m.at[1]); c1.start()
        c2=pltpu.make_async_copy(upb,up_ref,sem_m.at[2]); c2.start()
        outs+=[c1,c2]
    for co in outs: co.wait()

def final1(names, di, bh, bl, rs, cs, share_len, ndp):
    srows=sizes(share_len); n=len([x for g in names for x in g]); rows=sum(c.shape[0] for c in cs); ng=len(cs)
    return pl.pallas_call(functools.partial(final_kernel,names,share_len,srows,ndp,None),
        out_shape=(jax.ShapeDtypeStruct((FROWS,128),f32),jax.ShapeDtypeStruct((srows+2*BLK+16,128),f32)),
        in_specs=[SM]+[VM]*(3+ng), out_specs=(ANY,VM),
        scratch_shapes=[V((2,48,1152),bf),V((8,QCOLS),f32),V((rows,128),f32),pltpu.SemaphoreType.DMA((n,))],
        compiler_params=pltpu.CompilerParams(vmem_limit_bytes=rows*512+5*2**20),name="final1")(di,bh,bl,rs,*cs)
def final2(names, names1, di, bh, bl, rs, cs, rs1, psum, vcol, div, mom, ne, share, share_len, ndp):
    srows=sizes(share_len); n=len([x for g in names for x in g]); rows=sum(c.shape[0] for c in cs); ng=len(cs)
    return pl.pallas_call(functools.partial(final_kernel,names,share_len,srows,ndp,([x for g in names1 for x in g],vcol)),
        out_shape=(jax.ShapeDtypeStruct((FROWS,128),f32),jax.ShapeDtypeStruct((8,QCOLS),f32),jax.ShapeDtypeStruct((1,1),f32),jax.ShapeDtypeStruct((1,share_len),f32),jax.ShapeDtypeStruct((1,share_len),f32)),
        in_specs=[SM]+[VM]*(3+ng)+[VM,VM,VM,ANY,ANY,ANY], out_specs=(ANY,VM,VM,ANY,ANY),
        input_output_aliases={4+ng+4:0},
        scratch_shapes=[V(share.shape,f32),V((2,48,1152),bf),V((8,QCOLS),f32),V((rows,128),f32),pltpu.SemaphoreType.DMA((n,))]+[V((1,share_len),f32)]*3+[pltpu.SemaphoreType.DMA((4,))],
        compiler_params=pltpu.CompilerParams(vmem_limit_bytes=rows*512+share.shape[0]*512+12*share_len+5*2**20),name="final2")(di,bh,bl,rs,*cs,rs1,psum,div,mom,ne,share)
eps=1e-05
def sbytes(scr):
    t=0
    for x in scr:
        if not hasattr(x,"shape") or len(x.shape)<2: continue
        sh=list(x.shape); n=jnp.dtype(x.dtype).itemsize; sub=8*4//n
        sh[-1]+=(-sh[-1])%128; sh[-2]+=(-sh[-2])%sub
        k=n
        for y in sh: k*=y
        t+=k
    return t
def cp(mb,name,scr=()): return dict(scratch_shapes=list(scr),compiler_params=pltpu.CompilerParams(vmem_limit_bytes=sbytes(scr)+mb*2**20),name=name)
def S(*s): return jax.ShapeDtypeStruct(s,f32)
def rows(i,n=128): return pl.ds(pl.multiple_of(i*n,n),n)
def put2(h,l,v): a,b=split(v); h[...]=a; l[...]=b
def loop(n,f):
    def b(i,c):
        f(i); return c
    lax.fori_loop(0,n,b,0)
def ln_parts(v):
    c=v-jnp.mean(v,axis=-1,keepdims=True)
    inv=lax.rsqrt(jnp.mean(c*c,axis=-1,keepdims=True)+eps)
    return c*inv,inv
def ln_back(g,nrm,inv,gain):
    s=g*gain
    return inv*(s-jnp.mean(s,axis=-1,keepdims=True)-nrm*jnp.mean(s*nrm,axis=-1,keepdims=True))
def gelu(v): return 0.5*v*(1.0+lax.erf(v*0.7071067811865476))
def csum(v): return jnp.sum(v,axis=0,keepdims=True)
def mask_rows(mf_ref,i):
    r=iota((128,256),0)+i*128
    return jnp.max(jnp.where(mf_ref[0:1,:]==r,1.0,0.0),axis=1,keepdims=True)
def tn_grad(xh,xl,dh,dl,o_ref,ncol):
    def f(i):
        r=rows(i)
        o_ref[r,:]=d3((xh[:,r],xl[:,r]),(dh[...],dl[...]),TN)
    loop(ncol//128,f)

def put_half(rank_ref,i,keep,send,v):
    c=rank_ref[0]%2; r=rows(i%2)
    @pl.when(i//2==c)
    def _(): keep[r,:]=v
    @pl.when(i//2!=c)
    def _(): send[r,:]=v
def get_half(rank_ref,i,mine,peer):
    r=rows(i%2)
    return jnp.where(i//2==rank_ref[0]%2,mine[r,:],peer[r,:])
def get_full(rank_ref,i,ps):
    t=rank_ref[0]; r=rows(i); v=[p[r,:] for p in ps]
    return jnp.concatenate([jnp.where(t==s,v[0],jnp.where(t==s^1,v[1],jnp.where(t==s^2,v[2],v[3]))) for s in range(4)],axis=1)

def front_kernel(fr_ref,mf_ref,fn_ref,wf_ref,sb_ref,wq_ref,qb_ref,hid_ref,prob_ref,ps_ref,wfh,wfl,wqh,wql):
    put2(wfh,wfl,wf_ref[...]); put2(wqh,wql,wq_ref[...])
    ps_ref[...]=jnp.zeros_like(ps_ref)
    low=iota((128,640),1)<320
    def f(i):
        r=rows(i)
        nrm,_=ln_parts(fr_ref[r,:]); nd=nrm*fn_ref[0:1,:]+fn_ref[1:2,:]
        a=split(nd); m=mask_rows(mf_ref,i)
        hid=d3(a,(wfh[...],wfl[...]),NN)+sb_ref[1:2,:]
        hid_ref[r,:]=hid*(1.0-m)+m*sb_ref[0:1,:]
        lg=d3(a,(wqh[...],wql[...]),NN)+qb_ref[...]
        ninf=jnp.full_like(lg,-jnp.inf); z=jnp.zeros_like(lg)
        m0=jnp.max(jnp.where(low,lg,ninf),axis=1,keepdims=True); m1=jnp.max(jnp.where(low,ninf,lg),axis=1,keepdims=True)
        e=jnp.exp(lg-jnp.where(low,m0,m1))
        s0=jnp.sum(jnp.where(low,e,z),axis=1,keepdims=True); s1=jnp.sum(jnp.where(low,z,e),axis=1,keepdims=True)
        p=e*jnp.where(low,1.0/s0,1.0/s1)
        prob_ref[r,:]=p
        ps_ref[...]+=csum(p*m)
    loop(4,f)
def front(fr,mf,fn,wf,sb,wq,qb):
    return pl.pallas_call(front_kernel,out_shape=(S(512,768),S(512,640),S(1,640)),in_specs=[VM]*7,out_specs=(VM,)*3,
        **cp(6,"front",[V((512,768),bf)]*2+[V((512,640),bf)]*2))(fr,mf,fn,wf,sb,wq,qb)

def hist_kernel(ds_ref,mf_ref,cnt_ref,hs):
    def f(i):
        r=pl.ds(pl.multiple_of(i*64,64),64)
        c=iota((64,256),0)+i*64; acc=jnp.zeros((64,256),f32)
        for n in range(100):
            acc=acc+jnp.where(ds_ref[n:n+1,:]==c,1.0,0.0)
        hs[r,:]=acc.astype(bf)
    loop(8,f)
    def g(i):
        r=iota((128,256),0)+i*128
        oh=jnp.where(mf_ref[0:1,:]==r,1.0,0.0)
        k=jnp.max(oh,axis=1,keepdims=True)
        fr=iota((128,512),0)+i*128; co=iota((128,512),1)
        cnt_ref[rows(i),:]=d(oh.astype(bf),hs[...],NT)+jnp.where(fr==co,k,0.0)
    loop(4,g)
def hist(ds,mf):
    return pl.pallas_call(hist_kernel,out_shape=S(512,512),in_specs=[VM]*2,out_specs=VM,**cp(4,"hist",[V((512,256),bf)]))(ds,mf)

def attn_kernel(rank_ref,hid_ref,cv0,cv1,cv2,cv3,ng_ref,sb_ref,wq_ref,sp_ref,wo_ref,n0_ref,i0_ref,qkv_ref,w_ref,mx_ref,keep_ref,send_ref,wqh,wql,woh,wol,kvh,kvl):
    put2(wqh,wql,wq_ref[...]); put2(woh,wol,wo_ref[...])
    bias=jnp.concatenate([sp_ref[1:2,:],jnp.zeros((1,192),f32),sp_ref[2:3,:]],axis=1)
    def f(i):
        r=rows(i)
        nrm,inv=ln_parts(hid_ref[r,:]+get_full(rank_ref,i,(cv0,cv1,cv2,cv3)))
        n0_ref[r,:]=nrm; i0_ref[r,:]=inv
        x0=nrm*ng_ref[0:1,:]+sb_ref[2:3,:]
        v=d3(split(x0),(wqh[...],wql[...]),NT)+bias
        qkv_ref[r,:]=v
        a,b=split(v[:,192:576]); kvh[r,:]=a; kvl[r,:]=b
    loop(4,f)
    def g(i):
        r=rows(i); ms=[]
        for h in range(3):
            q=split(qkv_ref[r,64*h:64*h+64]*0.125)
            k=(kvh[:,64*h:64*h+64],kvl[:,64*h:64*h+64]); v=(kvh[:,192+64*h:256+64*h],kvl[:,192+64*h:256+64*h])
            s=d3(q,k,NT)
            e=jnp.exp(s-jnp.max(s,axis=1,keepdims=True))
            w=e*(1.0/jnp.sum(e,axis=1,keepdims=True))
            w_ref[h,r,:]=w
            ms.append(d3(split(w),v,NN))
        mx=jnp.concatenate(ms,axis=1)
        mx_ref[r,:]=mx
        put_half(rank_ref,i,keep_ref,send_ref,d3(split(mx),(woh[...],wol[...]),NN))
    loop(4,g)
def attn(rank,hid,cv,ng,sb,wq,qvb,wo):
    return pl.pallas_call(attn_kernel,out_shape=(S(512,768),S(512,1),S(512,576),S(3,512,512),S(512,192),S(256,768),S(256,768)),in_specs=[SM]+[VM]*10,out_specs=(VM,)*7,
        **cp(6,"attn",[V((576,768),bf)]*2+[V((192,768),bf)]*2+[V((512,384),bf)]*2))(rank,hid,*cv,ng,sb,wq,qvb,wo)

def ffn_kernel(rank_ref,n0_ref,am,ap,ng_ref,sb_ref,up_ref,ub_ref,dn_ref,n1_ref,i1_ref,u_ref,keep_ref,send_ref,uh,ul,dh,dl):
    put2(uh,ul,up_ref[...]); put2(dh,dl,dn_ref[...])
    def f(i):
        r=rows(i)
        x0=n0_ref[r,:]*ng_ref[0:1,:]+sb_ref[2:3,:]
        nrm,inv=ln_parts(x0+get_half(rank_ref,i,am,ap)+sb_ref[3:4,:])
        n1_ref[r,:]=nrm; i1_ref[r,:]=inv
        x1=nrm*ng_ref[1:2,:]+sb_ref[4:5,:]
        u=d3(split(x1),(uh[...],ul[...]),NN)+ub_ref[...]
        u_ref[r,:]=u
        put_half(rank_ref,i,keep_ref,send_ref,d3(split(gelu(u)),(dh[...],dl[...]),NN))
    loop(4,f)
def ffn(rank,n0,as_,ng,sb,up,ub,dn):
    return pl.pallas_call(ffn_kernel,out_shape=(S(512,768),S(512,1),S(512,768),S(256,768),S(256,768)),in_specs=[SM]+[VM]*8,out_specs=(VM,)*5,
        **cp(6,"ffn",[V((768,768),bf)]*4))(rank,n0,*as_,ng,sb,up,ub,dn)

def onehot_t(id_ref, g, i):
    return jnp.where(id_ref[g:g+1,rows(i)]==iota((320,128),0),1.0,0.0).astype(bf)
def target_kernel(id_ref,bk_ref,tp_ref,hb_ref,q_ref,th_ref,it_ref,tph,tpl_):
    put2(tph,tpl_,tp_ref[...])
    b=[]
    for g in range(2):
        v=bk_ref[g]; h=v.astype(bf); r1=v-h.astype(f32); m=r1.astype(bf); l=(r1-m.astype(f32)).astype(bf); b.append((h,m,l))
    def f(i):
        r=rows(i); qs=[]
        for g in range(2):
            o=onehot_t(id_ref,g,i)
            qs.append(d(o,b[g][0],TN)+(d(o,b[g][1],TN)+d(o,b[g][2],TN)))
        q=jnp.concatenate(qs,axis=1); q_ref[r,:]=q
        t=d3(split(q),(tph[...],tpl_[...]),NN)+hb_ref[1:2,:]
        it=lax.rsqrt(jnp.sum(t*t,axis=1,keepdims=True)+1e-6)
        it_ref[r,:]=it; th_ref[r,:]=t*it
    loop(4,f)
def target(ids,bk,tp,hb):
    return pl.pallas_call(target_kernel,out_shape=(S(512,256),S(512,256),S(512,1)),in_specs=[VM]*4,out_specs=(VM,)*3,**cp(6,"target",[V((256,256),bf)]*2))(ids,bk,tp,hb)

def head_kernel(rank_ref,n1_ref,fm,fp,mf_ref,ng_ref,sb_ref,hp_ref,hb_ref,cnt_ref,th_ref,
                loss_ref,pre_ref,vec_ref,gh_ref,ghb_ref,dth_ref, hph,hpl,thh,thl,xh,xl,dph,dpl,gmh,gml,phh,phl):
    put2(hph,hpl,hp_ref[...]); put2(thh,thl,th_ref[...])
    loss_ref[...]=jnp.zeros_like(loss_ref); vec_ref[...]=jnp.zeros_like(vec_ref); ghb_ref[...]=jnp.zeros_like(ghb_ref)
    def f(i):
        r=rows(i)
        x1=n1_ref[r,:]*ng_ref[1:2,:]+sb_ref[4:5,:]
        nrm,inv=ln_parts(x1+get_half(rank_ref,i,fm,fp)+sb_ref[5:6,:])
        x2=split(nrm*ng_ref[2:3,:]+sb_ref[6:7,:])
        xh[r,:]=x2[0]; xl[r,:]=x2[1]
        p=d3(x2,(hph[...],hpl[...]),NN)+hb_ref[0:1,:]
        ip=lax.rsqrt(jnp.sum(p*p,axis=1,keepdims=True)+1e-6)
        ph=p*ip; ps=split(ph); phh[r,:]=ps[0]; phl[r,:]=ps[1]
        s=d3(ps,(thh[...],thl[...]),NT)*10.0
        m=mask_rows(mf_ref,i)
        e=cnt_ref[r,:]*jnp.exp(s)
        z=jnp.sum(e,axis=1,keepdims=True); z=jnp.where(m>0.0,z,1.0)
        eye=iota((128,512),0)+i*128==iota((128,512),1)
        diag=jnp.sum(jnp.where(eye,s,0.0),axis=1,keepdims=True)
        loss_ref[...]+=jnp.sum(m*(jnp.log(z)-diag),axis=0,keepdims=True)
        g=(e*(1.0/z)-jnp.where(eye,m,0.0))*10.0
        gs=split(g); gmh[r,:]=gs[0]; gml[r,:]=gs[1]
        dp=d3(gs,(thh[...],thl[...]),NN)
        dpred=ip*(dp-ph*jnp.sum(dp*ph,axis=1,keepdims=True))
        ghb_ref[...]+=csum(dpred)
        ds=split(dpred); dph[r,:]=ds[0]; dpl[r,:]=ds[1]
        dx=d3(ds,(hph[...],hpl[...]),NT)
        vec_ref[0:1,:]+=csum(dx*nrm); vec_ref[1:2,:]+=csum(dx)
        pre=ln_back(dx,nrm,inv,ng_ref[2:3,:])
        pre_ref[r,:]=pre; vec_ref[2:3,:]+=csum(pre)
    loop(4,f)
    tn_grad(xh,xl,dph,dpl,gh_ref,768)
    tn_grad(gmh,gml,phh,phl,dth_ref,512)
def head(rank,n1,fs,mf,ng,sb,hp,hb,cnt,th):
    return pl.pallas_call(head_kernel,out_shape=(S(1,1),S(512,768),S(3,768),S(768,256),S(1,256),S(512,256)),in_specs=[SM]+[VM]*10,out_specs=(VM,)*6,
        **cp(6,"head",[V((768,256),bf)]*2+[V((512,256),bf)]*2+[V((512,768),bf)]*2+[V((512,256),bf)]*2+[V((512,512),bf)]*2+[V((512,256),bf)]*2))(rank,n1,*fs,mf,ng,sb,hp,hb,cnt,th)

def tback_kernel(dth_ref,th_ref,it_ref,q_ref,id_ref,tp_ref,gt_ref,ghb_ref,gb_ref,tph,tpl_,qh,ql,dth,dtl):
    put2(tph,tpl_,tp_ref[...]); put2(qh,ql,q_ref[...])
    ghb_ref[...]=jnp.zeros_like(ghb_ref); gb_ref[...]=jnp.zeros_like(gb_ref)
    def f(i):
        r=rows(i); g=dth_ref[r,:]; th=th_ref[r,:]
        dt=it_ref[r,:]*(g-th*jnp.sum(g*th,axis=1,keepdims=True))
        ghb_ref[...]+=csum(dt)
        ds=split(dt); dth[r,:]=ds[0]; dtl[r,:]=ds[1]
        dq=d3(ds,(tph[...],tpl_[...]),NT)
        for k in range(2):
            o=onehot_t(id_ref,k,i); a,b=split(dq[:,128*k:128*k+128])
            gb_ref[320*k:320*k+320,:]+=d(o,a,NN)+d(o,b,NN)
    loop(4,f)
    tn_grad(qh,ql,dth,dtl,gt_ref,256)
def tback(dth,th,it,q,ids,tp):
    return pl.pallas_call(tback_kernel,out_shape=(S(256,256),S(1,256),S(640,128)),in_specs=[VM]*6,out_specs=(VM,)*3,
        **cp(6,"tback",[V((256,256),bf)]*2+[V((512,256),bf)]*4))(dth,th,it,q,ids,tp)

def ffnb_kernel(rank_ref,pre_ref,u_ref,up_ref,dn_ref,du_ref,ub_ref,keep_ref,send_ref,uh,ul,dh,dl):
    put2(uh,ul,up_ref[...]); put2(dh,dl,dn_ref[...])
    ub_ref[...]=jnp.zeros_like(ub_ref)
    def f(i):
        r=rows(i)
        du=d3(split(pre_ref[r,:]),(dh[...],dl[...]),NT)*gelu_grad(u_ref[r,:])
        du_ref[r,:]=du; ub_ref[...]+=csum(du)
        put_half(rank_ref,i,keep_ref,send_ref,d3(split(du),(uh[...],ul[...]),NT))
    loop(4,f)
def ffnb(rank,pre,u,up,dn):
    return pl.pallas_call(ffnb_kernel,out_shape=(S(512,768),S(1,768),S(256,768),S(256,768)),in_specs=[SM]+[VM]*4,out_specs=(VM,)*4,
        **cp(6,"ffnb",[V((768,768),bf)]*4))(rank,pre,u,up,dn)
def ffnw_kernel(n1_ref,ng_ref,sb_ref,u_ref,du_ref,pre_ref,gu_ref,gd_ref,ah,al,bh,bl):
    put2(ah,al,n1_ref[...]*ng_ref[1:2,:]+sb_ref[4:5,:]); put2(bh,bl,du_ref[...])
    tn_grad(ah,al,bh,bl,gu_ref,768)
    put2(ah,al,gelu(u_ref[...])); put2(bh,bl,pre_ref[...])
    tn_grad(ah,al,bh,bl,gd_ref,768)
def ffnw(n1,ng,sb,u,du,pre):
    return pl.pallas_call(ffnw_kernel,out_shape=(S(768,768),S(768,768)),in_specs=[VM]*6,out_specs=(VM,)*2,
        **cp(6,"ffnw",[V((512,768),bf)]*4))(n1,ng,sb,u,du,pre)

def attnb_kernel(rank_ref,pre2_ref,fbm,fbp,n1_ref,i1_ref,ng_ref,wo_ref,qkv_ref,w_ref,wq_ref,pre_ref,vec_ref,dqkv_ref,keep_ref,send_ref,woh,wol,wqh,wql,qh,ql,dmh,dml,dsh,dsl):
    put2(woh,wol,wo_ref[...]); put2(wqh,wql,wq_ref[...]); put2(qh,ql,qkv_ref[...])
    vec_ref[...]=jnp.zeros_like(vec_ref)
    def f(i):
        r=rows(i)
        g=pre2_ref[r,:]+get_half(rank_ref,i,fbm,fbp); nrm=n1_ref[r,:]
        vec_ref[0:1,:]+=csum(g*nrm); vec_ref[1:2,:]+=csum(g)
        pre=ln_back(g,nrm,i1_ref[r,:],ng_ref[1:2,:])
        pre_ref[r,:]=pre; vec_ref[2:3,:]+=csum(pre)
        a,b=split(d3(split(pre),(woh[...],wol[...]),NT))
        dmh[r,:]=a; dml[r,:]=b
    loop(4,f)
    dvs=[];dks=[]
    for h in range(3):
        hs=slice(64*h,64*h+64); ks=slice(192+64*h,256+64*h); vs=slice(384+64*h,448+64*h)
        def g(i,c):
            r=rows(i)
            w=w_ref[h,r,:]
            dm=(dmh[r,hs],dml[r,hs])
            dw=d3(dm,(qh[:,vs],ql[:,vs]),NT)
            s=w*(dw-jnp.sum(dw*w,axis=1,keepdims=True))*0.125
            ss=split(s)
            dsh[r,:]=ss[0]; dsl[r,:]=ss[1]
            dqkv_ref[r,hs]=d3(ss,(qh[:,ks],ql[:,ks]),NN)
            return c+d3(split(w),dm,TN)
        dvs.append(lax.fori_loop(0,4,g,jnp.zeros((512,64),f32)))
        dks.append(d3((dsh[...],dsl[...]),(qh[:,hs],ql[:,hs]),TN))
    dqkv_ref[:,192:576]=jnp.concatenate(dks+dvs,axis=1)
    def p(i):
        r=rows(i)
        put_half(rank_ref,i,keep_ref,send_ref,d3(split(dqkv_ref[r,:]),(wqh[...],wql[...]),NN))
    loop(4,p)
def attnb(rank,pre2,fb,n1,i1,ng,wo,qkv,w,wq):
    return pl.pallas_call(attnb_kernel,out_shape=(S(512,768),S(3,768),S(512,576),S(256,768),S(256,768)),in_specs=[SM]+[VM]*10,out_specs=(VM,)*5,
        **cp(6,"attnb",[V((192,768),bf)]*2+[V((576,768),bf)]*2+[V((512,576),bf)]*2+[V((512,192),bf)]*2+[V((512,512),bf)]*2))(rank,pre2,*fb,n1,i1,ng,wo,qkv,w,wq)
def attnw_kernel(n0_ref,ng_ref,sb_ref,dqkv_ref,mx_ref,pre_ref,gq_ref,go_ref,b_ref,ah,al,bh,bl,mh,ml,ph,pl_):
    put2(ah,al,n0_ref[...]*ng_ref[0:1,:]+sb_ref[2:3,:]); put2(bh,bl,dqkv_ref[...])
    b_ref[...]=csum(dqkv_ref[...])
    tn_grad(ah,al,bh,bl,gq_ref,768)
    put2(mh,ml,mx_ref[...]); put2(ph,pl_,pre_ref[...])
    go_ref[...]=d3((mh[...],ml[...]),(ph[...],pl_[...]),TN)
def attnw(n0,ng,sb,dqkv,mx,pre):
    return pl.pallas_call(attnw_kernel,out_shape=(S(768,576),S(192,768),S(1,576)),in_specs=[VM]*6,out_specs=(VM,)*3,
        **cp(6,"attnw",[V((512,768),bf)]*2+[V((512,576),bf)]*2+[V((512,192),bf)]*2+[V((512,768),bf)]*2))(n0,ng,sb,dqkv,mx,pre)

def conv_bd_kernel(rank_ref,pre1_ref,am,ap,n0_ref,i0_ref,ng_ref,pre_ref,w8h,w8l,pre0_ref,vec_ref,gx_ref,dy_ref,gb_ref,own,dp,dyh,dyl,tp):
    vec_ref[...]=jnp.zeros_like(vec_ref)
    sel=sel_own(rank_ref[0],768)
    def f(i):
        r=rows(i)
        g=pre1_ref[r,:]+get_half(rank_ref,i,am,ap); nrm=n0_ref[r,:]
        vec_ref[0:1,:]+=csum(g*nrm); vec_ref[1:2,:]+=csum(g)
        p=ln_back(g,nrm,i0_ref[r,:],ng_ref[0:1,:])
        pre0_ref[r,:]=p
        h,l=split(p); own[r,:]=d(h,sel,NN)+d(l,sel,NN)
    loop(4,f)
    l512=iota((512,128),1)
    pres=from_natural(pre_ref[:,0:128],pre_ref[:,128:192])
    dp[0:16,:]=jnp.zeros((16,256),f32); dp[528:560,:]=jnp.zeros((32,256),f32)
    tp[0:64,:]=jnp.zeros((64,512),f32); tp[592:640,:]=jnp.zeros((48,512),f32)
    dxs=[];gbs=[]
    for g in range(4):
        a=own[:,128*(g//2):128*(g//2)+128]
        if g%2: a=roll(a,64)
        dy=jnp.where(l512<48,a*gelu_grad(pres[g]),0.0)
        gbs.append(jnp.sum(dy,axis=0,keepdims=True))
        dy_ref[g]=dy
        fine_col(dy,dp,dyh,dyl)
        def body(i,c):
            r=pl.ds(m8(i*176,16),176)
            tp[pl.ds(m8(64+i*176,16),176),:]=d3((dyh[r,:],dyl[r,:]),(w8h[g],w8l[g]),NT)
            return c
        lax.fori_loop(0,3,body,0)
        u=jnp.zeros((512,128),f32); v=u
        for j in range(4):
            u=u+tp[128-32*j:640-32*j,j*128:(j+1)*128]
            v=v+tp[112-32*j:624-32*j,j*128:(j+1)*128]
        dxs.append(u+roll(v,64))
    t0,t1=to_natural(dxs)
    gx_ref[:,0:128]=t0; gx_ref[:,128:192]=t1
    t0,t1=to_natural([jnp.broadcast_to(x,(8,128)) for x in gbs])
    gb_ref[:,0:128]=t0[0:1]; gb_ref[:,128:192]=t1[0:1]
def fine_col(dy,dp,dyh,dyl):
    dp[16:528,0:128]=dy
    dp[17:529,128:256]=roll(dy,64)
    dp[16:17,128:256]=jnp.zeros((1,128),f32)
    for j in range(8):
        v=dp[16-2*j:16-2*j+528,0:128]+dp[16-2*j:16-2*j+528,128:256]
        a,b=split(v)
        dyh[:,j*128:(j+1)*128]=a; dyl[:,j*128:(j+1)*128]=b
def conv_bd(rank,pre1,as_,n0,i0,ng,pre,w8h,w8l):
    return pl.pallas_call(conv_bd_kernel,out_shape=(S(512,768),S(2,768),S(512,192),S(4,512,128),S(1,192)),in_specs=[SM]+[VM]*9,out_specs=(VM,)*5,
        **cp(4,"conv_bd",[V((512,256),f32),V((560,256),f32)]+[V((528,1024),bf)]*2+[V((640,512),f32)]))(rank,pre1,*as_,n0,i0,ng,pre,w8h,w8l)
def conv_bw_kernel(rank_ref,hid_ref,dy_ref,gw_ref,xph,xpl,colh,coll,dp,dyh,dyl,dw8):
    sel=sel_own(rank_ref[0],768)
    h,l=split(hid_ref[...])
    zero_pad(xph); zero_pad(xpl)
    place_pairs(d(h,sel,NN),xph); place_pairs(d(l,sel,NN),xpl)
    dp[0:16,:]=jnp.zeros((16,256),f32); dp[528:560,:]=jnp.zeros((32,256),f32)
    for g in range(4):
        fine_col(dy_ref[g],dp,dyh,dyl)
        build_col(xph,g,colh); build_col(xpl,g,coll)
        def wbody(i,c):
            r=pl.ds(m8(i*128,128),128)
            dw8[g,r,:]=d3((colh[:,r],coll[:,r]),(dyh[...],dyl[...]),TN)
            return c
        lax.fori_loop(0,4,wbody,0)
    def nbody(m,c):
        for j in range(8):
            ps=[dw8[g,pl.ds(m8(m*64,16),48),j*128:(j+1)*128] for g in range(4)]
            t0,t1=to_natural(ps)
            r=pl.ds(m8((m*16+2*j)*48,16),48)
            gw_ref[r,0:128]=t0; gw_ref[r,128:192]=t1
            t0,t1=to_natural([roll(p,64) for p in ps])
            r=pl.ds(m8((m*16+2*j+1)*48,16),48)
            gw_ref[r,0:128]=t0; gw_ref[r,128:192]=t1
        return c
    lax.fori_loop(0,8,nbody,0)
def conv_bw(rank,hid,dy):
    return pl.pallas_call(conv_bw_kernel,out_shape=S(6144,192),in_specs=[SM,VM,VM],out_specs=VM,
        **cp(4,"conv_bw",[V((8,640,128),bf)]*2+[V((528,512),bf)]*2+[V((560,256),f32)]+[V((528,1024),bf)]*2+[V((4,512,1024),f32)]))(rank,hid,dy)

def quantb_kernel(total,fr_ref,mf_ref,fn_ref,wq_ref,prob_ref,tot_ref,gq_ref,gqb_ref,dn_ref,div_ref,wqh,wql,nh,nl,lh,ll):
    put2(wqh,wql,wq_ref[...])
    gqb_ref[...]=jnp.zeros_like(gqb_ref)
    mean=tot_ref[...]*(1.0/total); lo1=iota((1,640),1)<320; m1=mean+1e-07; lm=jnp.log(m1); t1=mean*lm; z1=jnp.zeros_like(t1)
    p0=jnp.exp(-jnp.sum(jnp.where(lo1,t1,z1),axis=1,keepdims=True)); p1=jnp.exp(-jnp.sum(jnp.where(lo1,z1,t1),axis=1,keepdims=True))
    div_ref[...]=(0.1*total/640.0)*(640.0-(p0+p1))
    dgr=(0.1/640.0)*jnp.where(lo1,p0,p1)*(lm+mean/m1)
    low=iota((128,640),1)<320
    def f(i):
        r=rows(i)
        nrm,_=ln_parts(fr_ref[r,:]); a,b=split(nrm*fn_ref[0:1,:]+fn_ref[1:2,:]); nh[r,:]=a; nl[r,:]=b
        m=mask_rows(mf_ref,i)
        p=prob_ref[r,:]; t=p*(m*dgr); z=jnp.zeros_like(t)
        s0=jnp.sum(jnp.where(low,t,z),axis=1,keepdims=True); s1=jnp.sum(jnp.where(low,z,t),axis=1,keepdims=True)
        lg=t-p*jnp.where(low,s0,s1)
        gqb_ref[...]+=csum(lg)
        y=split(lg); lh[r,:]=y[0]; ll[r,:]=y[1]
        dn_ref[r,:]=d3(y,(wqh[...],wql[...]),NT)
    loop(4,f)
    tn_grad(nh,nl,lh,ll,gq_ref,512)
def quantb(total,fr,mf,fn,wq,prob,dg):
    return pl.pallas_call(functools.partial(quantb_kernel,total),out_shape=(S(512,640),S(1,640),S(512,512),S(1,1)),in_specs=[VM]*6,out_specs=(VM,)*4,
        **cp(6,"quantb",[V((512,640),bf)]*2+[V((512,512),bf)]*2+[V((512,640),bf)]*2))(fr,mf,fn,wq,prob,dg)
def frontb_kernel(rank_ref,pre0_ref,c0,c1,c2,c3,fr_ref,mf_ref,fn_ref,wf_ref,dn_ref,gw_ref,gm_ref,gfn_ref,wfh,wfl,nh,nl,dh,dl):
    put2(wfh,wfl,wf_ref[...])
    gm_ref[...]=jnp.zeros_like(gm_ref); gfn_ref[...]=jnp.zeros_like(gfn_ref)
    def f(i):
        r=rows(i)
        nrm,_=ln_parts(fr_ref[r,:]); a,b=split(nrm*fn_ref[0:1,:]+fn_ref[1:2,:]); nh[r,:]=a; nl[r,:]=b
        m=mask_rows(mf_ref,i)
        gh=pre0_ref[r,:]+get_full(rank_ref,i,(c0,c1,c2,c3))
        dhd=gh*(1.0-m)
        gm_ref[0:1,:]+=csum(gh*m); gm_ref[1:2,:]+=csum(dhd)
        x=split(dhd); dh[r,:]=x[0]; dl[r,:]=x[1]
        dn=d3(x,(wfh[...],wfl[...]),NT)+dn_ref[r,:]
        gfn_ref[0:1,:]+=csum(dn*nrm); gfn_ref[1:2,:]+=csum(dn)
    loop(4,f)
    tn_grad(nh,nl,dh,dl,gw_ref,512)
def frontb(rank,pre0,cg,fr,mf,fn,wf,dn):
    return pl.pallas_call(frontb_kernel,out_shape=(S(512,768),S(2,768),S(2,512)),in_specs=[SM]+[VM]*10,out_specs=(VM,)*3,
        **cp(6,"frontb",[V((512,768),bf)]*2+[V((512,512),bf)]*2+[V((512,768),bf)]*2))(rank,pre0,*cg,fr,mf,fn,wf,dn)
from jax.sharding import PartitionSpec as P
G1=("out","up","down","hproj","tproj","book","qkv","quant"); GC=("conv",); GF=("feature",)

def swap(x,axis,bit):
    n=lax.axis_size(axis)
    return lax.ppermute(x,axis,[(i,i^bit) for i in range(n)])
def tie(x,y): return lax.optimization_barrier((x,y))[0]
def tsum(keep,send,fill=None):
    h=keep+swap(send,"tensor",1)
    o=swap(h,"tensor",2); out=None
    if fill:
        out=fill(h)
        o,out=lax.optimization_barrier((o,out))
    h=h+o
    return (h,swap(h,"tensor",1)),out
def tgather(x,fill):
    xo=swap(x,"tensor",2); co=swap(x,"tensor",1)
    out=fill(x)
    xo,out=lax.optimization_barrier((xo,out))
    return (x,co,xo,swap(xo,"tensor",1)),out
def dsum(x,fills=()):
    b=1; i=0; outs=[]
    while b<lax.axis_size("dp"):
        o=swap(x,"dp",b)
        if i<len(fills):
            out=fills[i](x)
            o,out=lax.optimization_barrier((o,out)); outs.append(out)
        x=x+o; b*=2; i+=1
    for f in fills[i:]: outs.append(f(x))
    return (x,outs) if fills else x

def shards(frames, masked_frames, distractors, code_ids, feature_weight, conv_weight, qkv_weight, out_weight, up_weight, down_weight,
           hidden_proj, target_proj, codebook, quant_weight, norm_gains, shared_bias, split_bias, up_bias, feature_norm, head_bias, quant_bias,
           momentum, error_buffer, factors):
    dp=lax.axis_size("dp"); total=256*dp
    rank=lax.axis_index("tensor").astype(jnp.int32).reshape(1); di=lax.axis_index("dp").astype(jnp.int32).reshape(1)
    ids=jnp.transpose(code_ids[0]); ds=jnp.transpose(distractors[0])
    wqkv=jnp.transpose(qkv_weight,(1,2,0)).reshape(576,768); w2=conv_weight.reshape(6144,192)
    fr,rank,di,ub,qb,w2=lax.optimization_barrier((frames[0],rank,di,up_bias[None],quant_bias[None],w2))
    mf=masked_frames; ng=norm_gains; sb=shared_bias; sp=split_bias
    hid,prob,psum_=front(fr,mf,feature_norm,feature_weight,sb,quant_weight,qb)
    prob_total=dsum(psum_)
    pre,cout,w8h,w8l=conv_fwd(rank,hid,w2,sp)
    cfull,((quant,th,it),cnt)=tgather(cout,lambda h:(target(ids,tie(codebook,h),target_proj,head_bias),hist(tie(ds,h),mf)))
    n0,i0,qkv,wts,mx,*ap=attn(rank,hid,cfull,ng,sb,wqkv,sp,out_weight)
    asum,(gqw,gqb,dnq,div)=tsum(*ap,lambda h: quantb(total,tie(fr,h),mf,feature_norm,quant_weight,prob,prob_total))
    n1,i1,u,*fp=ffn(rank,n0,asum,ng,sb,up_weight,ub,down_weight)
    fsum,_=tsum(*fp)
    lp,pre2,vec2,ghp,ghb0,dth=head(rank,n1,fsum,mf,ng,sb,hidden_proj,head_bias,cnt,th)
    du,gub,*bp=ffnb(rank,pre2,u,up_weight,down_weight)
    def fill3(h):
        return tback(tie(dth,h),th,it,quant,ids,target_proj),ffnw(n1,ng,sb,u,tie(du,h),pre2)
    bsum,((gtp,ghb1,gbook),(gup,gdn))=tsum(*bp,fill3)
    pre1,vec1,dqkv,*bp2=attnb(rank,pre2,bsum,n1,i1,ng,out_weight,qkv,wts,wqkv)
    ef=error_buffer.reshape(FROWS,128); fac=factors[0]
    gr={"up":gup,"down":gdn,"hproj":ghp,"tproj":gtp,"book":gbook,"quant":gqw}
    def fill4(h):
        gqkv,gout,gqb3=attnw(n0,ng,sb,tie(dqkv,h),mx,pre1)
        gr.update(qkv=gqkv,out=gout)
        return gqb3,left(G1,fac,ef,[gr[x] for x in G1])
    bsum2,(gqb3,(c1,p1))=tsum(*bp2,fill4)
    o=swap(p1,"dp",1)
    bd=conv_bd(rank,tie(pre1,p1),bsum2,n0,i0,ng,pre,w8h,w8l)
    o,(pre0,vec0,gx,dy,gcb)=lax.optimization_barrier((o,bd))
    x1=p1+o
    cg,gw=tgather(gx,lambda h: conv_bw(rank,hid,tie(dy,h)))
    s1=x1; b=2
    while b<dp:
        s1=s1+swap(s1,"dp",b); b*=2
    cc,pc=left(GC,fac,ef,[gw])
    o=swap(pc,"dp",1)
    gfw,gm,gfn=frontb(rank,tie(pre0,pc),cg,fr,mf,feature_norm,feature_weight,dnq)
    cf,pf=left(GF,fac,ef,[gfw],(vec0,vec1,vec2,gm,gcb,gqb3,gub,gfn,ghb0,ghb1,gqb,lp))
    o,cf,pf=lax.optimization_barrier((o,cf,pf))
    sc=pc+o
    o=swap(sc,"dp",2)
    bh1,bl1,r1=right((G1,),(tie(s1,sc),),(c1,))
    rs1=dsum(r1)
    sf=dsum(pf)
    o,rs1,sf=lax.optimization_barrier((o,rs1,sf))
    sc=sc+o
    sl=momentum.shape[1]
    b=4; o=None
    ne=share=None
    while b<dp:
        o=swap(sc,"dp",b)
        if ne is None:
            ne,share=final1((G1,),di,bh1,bl1,tie(rs1,sc),(c1,),sl,dp)
            o,ne,share=lax.optimization_barrier((o,ne,share))
        sc=sc+o; b*=2
    bh2,bl2,r2=right((GC,GF),(sc,sf),(cc,cf))
    rs2=dsum(r2)
    ne,nf,loss,nm,upd=final2((GC,GF),(G1,),di,bh2,bl2,rs2,(cc,cf),rs1,sf,sf.shape[1]-VCOLS,div,momentum,ne,share,sl,dp)
    return loss[0,0],nm,upd,ne.reshape(1,1,-1),nf[None]

def solution(mesh):
    return jax.shard_map(shards,mesh=mesh,
        in_specs=(P("dp",None,None),P("dp",None),P("dp",None,None),P("dp",None,None),P(),P(None,None,"tensor"),P(None,None,"tensor"),P("tensor",None),P(None,"tensor"),P("tensor",None),
            P(),P(),P(),P(),P(),P(),P(None,"tensor"),P("tensor"),P(),P(),P(),P("tensor","dp"),P("dp","tensor",None),P("tensor",None,None)),
        out_specs=(P(),P("tensor","dp"),P("tensor","dp"),P("dp","tensor",None),P("tensor",None,None)),check_vma=False)
```
